1024 devices in a mesh: row: 32 (over z_lo, y), col: 32 (over x, z_hi, core).
Axes of the slice: x: 4, y: 8, z: 16 (z_hi: 4, z_lo: 4; z = z_hi * 4 + z_lo), core: 2. Of those that a mesh axis runs over, the one named last changes fastest.
Arguments:
- coeff: bfloat16 [12288, 12288], P('row', 'col'), may hold values from -6 to 6
- bank: bfloat16 [16, 384, 384], replicated, may hold values from -0.09375 to 0.09375
- alpha_tiles: int32 [32, 24], replicated, may hold values from 0 to 31
- alpha_blocks: int32 [32, 24], replicated, may hold values from 0 to 15
- alpha_count: int32 [32], replicated, may hold values from 2 to 24, as said below
- beta_tiles: int32 [32, 24], replicated, may hold values from 0 to 31
- beta_blocks: int32 [32, 24], replicated, may hold values from 0 to 15
- beta_count: int32 [32], replicated, may hold values from 2 to 24, as said below
Outputs:
- sigma: float32 [12288, 12288], P('row', 'col')
The draws below stay inside these ranges and needn't reach their ends.
Inputs may be any that keep to these rules, and one draw needn't show every extreme that they name: `alpha_count`: every value lies in 2 to 24; some tile has all 24 slots live. `beta_count`: every value lies in 2 to 24; some tile has all 24 slots live.
All inputs are finite; a program needn't handle non-finite values.
Results may differ from the reference program's by a relative error of at most 0.0003.
Values may be sent and summed in bfloat16 or wider, within the bound.
No kernel may reach another device: no remote copies, remote signals or barrier semaphores. Data moves between devices by JAX's collectives and lax.ppermute only.
A program may use at most 64 MiB of HBM per device.

```python
import jax
import jax.numpy as jnp
from jax import lax

TILE = 384
LIST = 24
BANK = 16
NA = 12288
NB = 12288
N_ROW = 32
N_COL = 32


def draw_alpha_count(key, part):
    values = jax.random.randint(jax.random.fold_in(key, 11), (N_ROW,), 2, LIST + 1)
    chosen = jax.random.randint(jax.random.fold_in(key, 12), (), 0, N_ROW)
    return values.at[chosen].set(LIST).astype(jnp.int32)


def draw_beta_count(key, part):
    values = jax.random.randint(jax.random.fold_in(key, 21), (N_COL,), 2, LIST + 1)
    chosen = jax.random.randint(jax.random.fold_in(key, 22), (), 0, N_COL)
    return values.at[chosen].set(LIST).astype(jnp.int32)


def set_ends(values, key, smallest, high):
    longest = values.shape.index(max(values.shape))
    spots = []
    for shift in (0, 1):
        where = [jax.random.randint(jax.random.fold_in(key, axis), (), 0, length) for axis, length in enumerate(values.shape)]
        where[longest] = (where[longest] + shift) % values.shape[longest]
        spots.append(tuple(where))
    return values.at[spots[0]].set(smallest).at[spots[1]].set(high)


def block_levels(rng, extent, pieces, smallest, largest):
    level = 1.0
    for dim, parts in pieces:
        steps = jax.random.uniform(jax.random.fold_in(jax.random.fold_in(rng, 6), dim), (parts,), jnp.float32, smallest / len(pieces), largest / len(pieces))
        level = level * jnp.repeat(jnp.exp(steps), extent[dim] // parts).reshape((-1,) + (1,) * (len(extent) - 1 - dim))
    return level


def noise(stream_key, shape, scale, limit, pieces=(), kind=jnp.bfloat16):
    drawn = scale * jax.random.normal(stream_key, shape, jnp.float32)
    if pieces:
        drawn = drawn * block_levels(stream_key, shape, pieces, -0.22, 0.18)
    return jnp.clip(drawn, -limit, limit).astype(kind)


def setup_inputs(seed: int = 0) -> dict:
    splits = jax.random.split(jax.random.key(seed), 9)
    return {
        "coeff": noise(splits[0], (NA, NB), 1.0, 6.0, ((0, 32), (1, 32))),
        "bank": noise(splits[1], (BANK, TILE, TILE), (TILE * LIST // 2) ** -0.5, 0.09375),
        "alpha_tiles": set_ends(jax.random.randint(splits[2], (N_ROW, LIST), 0, N_ROW), jax.random.fold_in(splits[2], 1), 0, N_ROW - 1).astype(jnp.int32),
        "alpha_blocks": set_ends(jax.random.randint(splits[3], (N_ROW, LIST), 0, BANK), jax.random.fold_in(splits[3], 1), 0, BANK - 1).astype(jnp.int32),
        "alpha_count": draw_alpha_count(jax.random.fold_in(splits[8], 71), 0),
        "beta_tiles": set_ends(jax.random.randint(splits[5], (N_COL, LIST), 0, N_COL), jax.random.fold_in(splits[5], 1), 0, N_COL - 1).astype(jnp.int32),
        "beta_blocks": set_ends(jax.random.randint(splits[6], (N_COL, LIST), 0, BANK), jax.random.fold_in(splits[6], 1), 0, BANK - 1).astype(jnp.int32),
        "beta_count": draw_beta_count(jax.random.fold_in(splits[8], 71), 0),
    }


def reference(coeff, bank, alpha_tiles, alpha_blocks, alpha_count, beta_tiles, beta_blocks, beta_count):
    def alpha_rows(tile_row):
        tiles = alpha_tiles[tile_row]
        blocks = alpha_blocks[tile_row]

        def add_slot(slot, total):
            start = (tiles[slot] * TILE).astype(jnp.int32)
            piece = lax.dynamic_slice_in_dim(coeff, start, TILE, 0)
            return total + jnp.dot(bank[blocks[slot]], piece, preferred_element_type=jnp.float32)

        return lax.fori_loop(0, alpha_count[tile_row], add_slot, jnp.zeros((TILE, NB), jnp.float32))

    def beta_cols(tile_col):
        tiles = beta_tiles[tile_col]
        blocks = beta_blocks[tile_col]

        def add_slot(slot, total):
            start = (tiles[slot] * TILE).astype(jnp.int32)
            piece = lax.dynamic_slice_in_dim(coeff, start, TILE, 1)
            return total + lax.dot_general(piece, bank[blocks[slot]], (((1,), (1,)), ((), ())), preferred_element_type=jnp.float32)

        return lax.fori_loop(0, beta_count[tile_col], add_slot, jnp.zeros((NA, TILE), jnp.float32))

    sigma_alpha = lax.map(alpha_rows, jnp.arange(N_ROW, dtype=jnp.int32)).reshape(NA, NB)
    sigma_beta = lax.map(beta_cols, jnp.arange(N_COL, dtype=jnp.int32))
    sigma_beta = jnp.transpose(sigma_beta, (1, 0, 2)).reshape(NA, NB)
    return sigma_alpha + sigma_beta
```

```python
import jax
import jax.numpy as jnp
from jax import lax
from jax.experimental import pallas as pl
from jax.experimental.pallas import tpu as pltpu
from jax.sharding import PartitionSpec as P

PAD = 16
STEP = 4


def mix_kernel(tiles, blocks, count, x_ref, bank_ref, out_ref, prod_ref):
    banks, tile, _ = bank_ref.shape
    lanes = x_ref.shape[0]
    rows, slots = tiles.shape
    x = x_ref[...]
    prod_ref[pl.ds(banks * lanes, PAD), :] = jnp.zeros((PAD, tile), jnp.float32)

    def multiply(b, carry):
        prod_ref[pl.ds(pl.multiple_of(b * lanes, lanes), lanes), :] = lax.dot_general(
            x, bank_ref[b], (((1,), (1,)), ((), ())), preferred_element_type=jnp.float32
        )
        return carry

    lax.fori_loop(0, banks, multiply, 0)

    def gather(r, carry):
        live = count[r]

        def add(group, total):
            for lane in range(STEP):
                slot = group * STEP + lane
                at = blocks[r, slot] * lanes + tiles[r, slot] * PAD
                at = jnp.where(slot < live, at, banks * lanes)
                total = total + prod_ref[pl.ds(pl.multiple_of(at, PAD), PAD), :]
            return total

        out_ref[r] = lax.fori_loop(
            0, (live + STEP - 1) // STEP, add, jnp.zeros((PAD, tile), jnp.float32)
        )
        return carry

    lax.fori_loop(0, rows, gather, 0)


def mix(pieces, bank, tiles, blocks, count):
    rows, _, tile = pieces.shape
    banks = bank.shape[0]
    vmem = pl.BlockSpec(memory_space=pltpu.VMEM)
    smem = pl.BlockSpec(memory_space=pltpu.SMEM)
    return pl.pallas_call(
        mix_kernel,
        out_shape=jax.ShapeDtypeStruct((rows, PAD, tile), jnp.float32),
        in_specs=[smem, smem, smem, vmem, vmem],
        out_specs=vmem,
        scratch_shapes=[pltpu.VMEM((banks * rows * PAD + PAD, tile), jnp.float32)],
    )(tiles, blocks, count, pieces.reshape(rows * PAD, tile), bank)


def split(piece, parts):
    tile = piece.shape[0]
    width = tile // parts
    return jnp.pad(piece.reshape(parts, width, tile), ((0, 0), (0, PAD - width), (0, 0)))


def join(parts, tile):
    return parts[:, : tile // parts.shape[0]].reshape(tile, tile)


def swap(pieces, axis):
    return lax.all_to_all(pieces, axis, 0, 0, tiled=True)


def local(coeff, bank, alpha_tiles, alpha_blocks, alpha_count, beta_tiles, beta_blocks, beta_count):
    tile = coeff.shape[0]
    n_row = lax.axis_size("row")
    n_col = lax.axis_size("col")
    beta_in = swap(split(coeff, n_col), "col")
    alpha_in = swap(split(coeff.T, n_row), "row")
    alpha_out = swap(mix(alpha_in, bank, alpha_tiles, alpha_blocks, alpha_count), "row")
    beta_out = swap(mix(beta_in, bank, beta_tiles, beta_blocks, beta_count), "col")
    return join(alpha_out, tile).T + join(beta_out, tile)


def solution(mesh):
    return jax.shard_map(
        local,
        mesh=mesh,
        in_specs=(P("row", "col"), P(), P(), P(), P(), P(), P(), P()),
        out_specs=P("row", "col"),
        check_vma=False,
    )
```

```python
import jax
import jax.numpy as jnp
from jax import lax
from jax.experimental import pallas as pl
from jax.experimental.pallas import tpu as pltpu
from jax.sharding import PartitionSpec as P

LANE = 128
PAD = 16
PAIR = 2
CHAINS = 2
ROOM = 24 << 20
VMEM = pl.BlockSpec(memory_space=pltpu.VMEM)
SMEM = pl.BlockSpec(memory_space=pltpu.SMEM)


def inside(x):
    return pltpu.with_memory_space_constraint(x, pltpu.VMEM)


def wire_rows(width, tile):
    return -(-(width * tile // LANE + 1) // 8) * 8


def pack_kernel(x_ref, out_ref, flip_ref, *, flip):
    parts, rows, _ = out_ref.shape
    tile = x_ref.shape[0]
    width = tile // parts
    used = width * tile // LANE
    x = x_ref[...]
    top = jnp.max(jnp.max(jnp.abs(x.astype(jnp.float32)), axis=0, keepdims=True), axis=1, keepdims=True)
    foot = jnp.broadcast_to(top, (rows - used, LANE)).astype(out_ref.dtype)
    if flip:
        flip_ref[...] = x.astype(jnp.float32).T.astype(x.dtype)
        src = flip_ref
    else:
        src = x_ref
    for t in range(parts):
        for block in range(tile // LANE):
            out_ref[t, block * width : (block + 1) * width, :] = src[
                t * width : (t + 1) * width, block * LANE : (block + 1) * LANE
            ]
        out_ref[t, used:, :] = foot


def pack(piece, parts, flip):
    tile = piece.shape[0]
    return pl.pallas_call(
        lambda *refs: pack_kernel(*refs, flip=flip),
        out_shape=jax.ShapeDtypeStruct((parts, wire_rows(tile // parts, tile), LANE), piece.dtype),
        in_specs=[VMEM],
        out_specs=VMEM,
        scratch_shapes=[pltpu.VMEM((tile, tile), piece.dtype)],
        compiler_params=pltpu.CompilerParams(vmem_limit_bytes=ROOM),
        name="pack_flip" if flip else "pack",
    )(piece)


def mix_kernel(places, cap, in_ref, bank_ref, out_ref, scale_ref, x_ref, prod_ref):
    banks, tile, _ = bank_ref.shape
    parts = in_ref.shape[0]
    width = tile // parts
    used = width * tile // LANE
    lanes = x_ref.shape[0]

    def unpack(t, top):
        x_ref[pl.ds(pl.multiple_of(t * PAD, PAD), PAD), :] = jnp.zeros((PAD, tile), x_ref.dtype)
        for block in range(tile // LANE):
            x_ref[pl.ds(pl.multiple_of(t * PAD, PAD), width), block * LANE : (block + 1) * LANE] = in_ref[
                t, block * width : (block + 1) * width, :
            ]
        return jnp.maximum(top, in_ref[t, used : used + 1, :].astype(jnp.float32))

    top = lax.fori_loop(0, parts, unpack, jnp.zeros((1, LANE), jnp.float32))
    scale = 32768.0 / jnp.maximum(top * cap[0], 1e-30)
    scale_ref[...] = 1.0 / scale
    prod_ref[pl.ds(banks * lanes, PAD), :] = jnp.zeros((PAD, tile), jnp.float32)

    for b in range(0, banks, PAIR):
        both = lax.dot_general(
            x_ref[...],
            bank_ref[b : b + PAIR].reshape(PAIR * tile, tile),
            (((1,), (1,)), ((), ())),
            preferred_element_type=jnp.float32,
        )
        for side in range(PAIR):
            prod_ref[pl.ds((b + side) * lanes, lanes), :] = both[:, side * tile : (side + 1) * tile]

    def gather(r, carry):
        totals = [None] * CHAINS
        for slot in range(places.shape[1]):
            piece = prod_ref[pl.ds(pl.multiple_of(places[r, slot], PAD), PAD), :]
            chain = slot % CHAINS
            totals[chain] = piece if totals[chain] is None else totals[chain] + piece
        total = sum(totals[1:], totals[0])
        for block in range(tile // LANE):
            out_ref[r, block * width : (block + 1) * width, :] = (
                total[:width, block * LANE : (block + 1) * LANE] * scale
            )
        return carry

    lax.fori_loop(0, parts, gather, 0)


def mix(pieces, bank, places, cap):
    parts, _, _ = pieces.shape
    banks, tile, _ = bank.shape
    out, unscale = pl.pallas_call(
        mix_kernel,
        out_shape=(
            jax.ShapeDtypeStruct((parts, tile // parts * tile // LANE, LANE), jnp.float32),
            jax.ShapeDtypeStruct((1, LANE), jnp.float32),
        ),
        in_specs=[SMEM, SMEM, VMEM, VMEM],
        out_specs=(VMEM, VMEM),
        scratch_shapes=[
            pltpu.VMEM((parts * PAD, tile), pieces.dtype),
            pltpu.VMEM((banks * parts * PAD + PAD, tile), jnp.float32),
        ],
        compiler_params=pltpu.CompilerParams(vmem_limit_bytes=ROOM),
        name="mix",
    )(places, cap, inside(pieces), bank)
    return out.astype(jnp.float16), unscale


def find(tiles, blocks, count, banks):
    rows, slots = tiles.shape
    at = blocks * (rows * PAD) + tiles * PAD
    return jnp.where(jnp.arange(slots) < count[:, None], at, banks * rows * PAD)


def join_kernel(alpha_ref, beta_ref, alpha_unit, beta_unit, out_ref, flip_ref):
    parts, _, _ = beta_ref.shape
    tile = out_ref.shape[0]
    width = tile // parts
    for t in range(parts):
        for block in range(tile // LANE):
            flip_ref[t * width : (t + 1) * width, block * LANE : (block + 1) * LANE] = alpha_ref[
                t, block * width : (block + 1) * width, :
            ]
    out_ref[...] = (flip_ref[...] * alpha_unit[0, 0]).T
    for t in range(parts):
        for block in range(tile // LANE):
            out_ref[t * width : (t + 1) * width, block * LANE : (block + 1) * LANE] += (
                beta_ref[t, block * width : (block + 1) * width, :] * beta_unit[0, 0]
            )


def join(alpha, beta, alpha_unit, beta_unit, tile):
    return pl.pallas_call(
        join_kernel,
        out_shape=jax.ShapeDtypeStruct((tile, tile), jnp.float32),
        in_specs=[VMEM, VMEM, SMEM, SMEM],
        out_specs=VMEM,
        scratch_shapes=[pltpu.VMEM((tile, tile), jnp.float32)],
        compiler_params=pltpu.CompilerParams(vmem_limit_bytes=ROOM),
        name="join",
    )(inside(alpha.astype(jnp.float32)), inside(beta.astype(jnp.float32)), alpha_unit, beta_unit)


def swap(pieces, axis):
    return lax.all_to_all(pieces, axis, 0, 0, tiled=True)


def local(coeff, bank, alpha_tiles, alpha_blocks, alpha_count, beta_tiles, beta_blocks, beta_count):
    tile = coeff.shape[0]
    banks = bank.shape[0]
    n_row = lax.axis_size("row")
    n_col = lax.axis_size("col")
    slots = alpha_tiles.shape[1]
    held = inside(bank)
    beta_in = swap(pack(coeff, n_col, False), "col")
    alpha_in = swap(pack(coeff, n_row, True), "row")
    cap = (jnp.max(jnp.abs(bank)).astype(jnp.float32) * (slots * tile)).reshape(1)
    alpha_at = find(alpha_tiles, alpha_blocks, alpha_count, banks)
    beta_at = find(beta_tiles, beta_blocks, beta_count, banks)
    alpha_mix, alpha_unit = mix(alpha_in, held, alpha_at, cap)
    alpha_out = swap(alpha_mix, "row")
    beta_mix, beta_unit = mix(beta_in, held, beta_at, cap)
    beta_out = swap(beta_mix, "col")
    return join(alpha_out, beta_out, alpha_unit, beta_unit, tile)


def solution(mesh):
    return jax.shard_map(
        local,
        mesh=mesh,
        in_specs=(P("row", "col"), P(), P(), P(), P(), P(), P(), P()),
        out_specs=P("row", "col"),
        check_vma=False,
    )
```

```python
import jax
import jax.numpy as jnp
from jax import lax
from jax.experimental import pallas as pl
from jax.experimental.pallas import tpu as pltpu
from jax.sharding import PartitionSpec as P

LANE = 128
PAD = 16
PAIR = 2
CHAINS = 2
ROOM = 24 << 20
VMEM = pl.BlockSpec(memory_space=pltpu.VMEM)
SMEM = pl.BlockSpec(memory_space=pltpu.SMEM)


def inside(x):
    return pltpu.with_memory_space_constraint(x, pltpu.VMEM)


def wire_rows(width, tile):
    return -(-(width * tile // LANE + 1) // 8) * 8


def pack_kernel(x_ref, out_ref, flip_ref, *, flip):
    parts, rows, _ = out_ref.shape
    tile = x_ref.shape[0]
    width = tile // parts
    used = width * tile // LANE
    x = x_ref[...]
    top = jnp.max(jnp.max(jnp.abs(x.astype(jnp.float32)), axis=0, keepdims=True), axis=1, keepdims=True)
    foot = jnp.broadcast_to(top, (rows - used, LANE)).astype(out_ref.dtype)
    if flip:
        flip_ref[...] = x.astype(jnp.float32).T.astype(x.dtype)
        src = flip_ref
    else:
        src = x_ref
    for t in range(parts):
        for block in range(tile // LANE):
            out_ref[t, block * width : (block + 1) * width, :] = src[
                t * width : (t + 1) * width, block * LANE : (block + 1) * LANE
            ]
        out_ref[t, used:, :] = foot


def pack(piece, parts, flip):
    tile = piece.shape[0]
    return pl.pallas_call(
        lambda *refs: pack_kernel(*refs, flip=flip),
        out_shape=jax.ShapeDtypeStruct((parts, wire_rows(tile // parts, tile), LANE), piece.dtype),
        in_specs=[VMEM],
        out_specs=VMEM,
        scratch_shapes=[pltpu.VMEM((tile, tile), piece.dtype)],
        compiler_params=pltpu.CompilerParams(vmem_limit_bytes=ROOM),
        name="pack_flip" if flip else "pack",
    )(piece)


def mix_kernel(places, cap, in_ref, bank_hbm, out_ref, scale_ref, x_ref, prod_ref, bank_ref, sems):
    banks, tile, _ = bank_ref.shape
    parts = in_ref.shape[0]
    width = tile // parts
    used = width * tile // LANE
    lanes = x_ref.shape[0]
    edges = [0, PAIR, banks // 2, banks]
    copies = {
        low: pltpu.make_async_copy(bank_hbm.at[pl.ds(low, high - low)], bank_ref.at[pl.ds(low, high - low)], sems.at[i])
        for i, (low, high) in enumerate(zip(edges[:-1], edges[1:]))
    }
    for copy in copies.values():
        copy.start()

    def unpack(t, top):
        x_ref[pl.ds(pl.multiple_of(t * PAD, PAD), PAD), :] = jnp.zeros((PAD, tile), x_ref.dtype)
        for block in range(tile // LANE):
            x_ref[pl.ds(pl.multiple_of(t * PAD, PAD), width), block * LANE : (block + 1) * LANE] = in_ref[
                t, block * width : (block + 1) * width, :
            ]
        return jnp.maximum(top, in_ref[t, used : used + 1, :].astype(jnp.float32))

    top = lax.fori_loop(0, parts, unpack, jnp.zeros((1, LANE), jnp.float32))
    scale = 32768.0 / jnp.maximum(top * cap[0], 1e-30)
    scale_ref[...] = 1.0 / scale
    prod_ref[pl.ds(banks * lanes, PAD), :] = jnp.zeros((PAD, tile), jnp.float32)

    for b in range(0, banks, PAIR):
        if b in copies:
            copies[b].wait()
        both = lax.dot_general(
            x_ref[...],
            bank_ref[b : b + PAIR].reshape(PAIR * tile, tile),
            (((1,), (1,)), ((), ())),
            preferred_element_type=jnp.float32,
        )
        for side in range(PAIR):
            prod_ref[pl.ds((b + side) * lanes, lanes), :] = both[:, side * tile : (side + 1) * tile]

    def gather(r, carry):
        totals = [None] * CHAINS
        for slot in range(places.shape[1]):
            piece = prod_ref[pl.ds(pl.multiple_of(places[r, slot], PAD), PAD), :]
            chain = slot % CHAINS
            totals[chain] = piece if totals[chain] is None else totals[chain] + piece
        total = sum(totals[1:], totals[0])
        for block in range(tile // LANE):
            out_ref[r, block * width : (block + 1) * width, :] = (
                total[:width, block * LANE : (block + 1) * LANE] * scale
            )
        return carry

    lax.fori_loop(0, parts, gather, 0)


def mix(pieces, bank, places, cap):
    parts, _, _ = pieces.shape
    banks, tile, _ = bank.shape
    out, unscale = pl.pallas_call(
        mix_kernel,
        out_shape=(
            jax.ShapeDtypeStruct((parts, tile // parts * tile // LANE, LANE), jnp.float32),
            jax.ShapeDtypeStruct((1, LANE), jnp.float32),
        ),
        in_specs=[SMEM, SMEM, VMEM, pl.BlockSpec(memory_space=pltpu.HBM)],
        out_specs=(VMEM, VMEM),
        scratch_shapes=[
            pltpu.VMEM((parts * PAD, tile), pieces.dtype),
            pltpu.VMEM((banks * parts * PAD + PAD, tile), jnp.float32),
            pltpu.VMEM(bank.shape, bank.dtype),
            pltpu.SemaphoreType.DMA((3,)),
        ],
        compiler_params=pltpu.CompilerParams(vmem_limit_bytes=ROOM),
        name="mix",
    )(places, cap, inside(pieces), pltpu.with_memory_space_constraint(bank, pltpu.HBM))
    return out.astype(jnp.float16), unscale


def find(tiles, blocks, count, banks):
    rows, slots = tiles.shape
    at = blocks * (rows * PAD) + tiles * PAD
    return jnp.where(jnp.arange(slots) < count[:, None], at, banks * rows * PAD)


def turn_kernel(parts_ref, unit, out_ref, flip_ref):
    parts = parts_ref.shape[0]
    tile = out_ref.shape[0]
    width = tile // parts
    for t in range(parts):
        for block in range(tile // LANE):
            flip_ref[t * width : (t + 1) * width, block * LANE : (block + 1) * LANE] = parts_ref[
                t, block * width : (block + 1) * width, :
            ]
    out_ref[...] = flip_ref[...].T * unit[0, 0]


def turn(parts, unit, tile):
    return pl.pallas_call(
        turn_kernel,
        out_shape=jax.ShapeDtypeStruct((tile, tile), jnp.float32),
        in_specs=[VMEM, SMEM],
        out_specs=VMEM,
        scratch_shapes=[pltpu.VMEM((tile, tile), jnp.float32)],
        compiler_params=pltpu.CompilerParams(vmem_limit_bytes=ROOM),
        name="turn",
    )(inside(parts.astype(jnp.float32)), unit)


def join_kernel(base_ref, parts_ref, unit, out_ref):
    parts = parts_ref.shape[0]
    tile = out_ref.shape[0]
    width = tile // parts
    for t in range(parts):
        for block in range(tile // LANE):
            rows, cols = slice(t * width, (t + 1) * width), slice(block * LANE, (block + 1) * LANE)
            out_ref[rows, cols] = base_ref[rows, cols] + parts_ref[t, block * width : (block + 1) * width, :] * unit[0, 0]


def join(base, parts, unit):
    return pl.pallas_call(
        join_kernel,
        out_shape=jax.ShapeDtypeStruct(base.shape, jnp.float32),
        in_specs=[VMEM, VMEM, SMEM],
        out_specs=VMEM,
        compiler_params=pltpu.CompilerParams(vmem_limit_bytes=ROOM),
        name="join",
    )(inside(base), inside(parts.astype(jnp.float32)), unit)


def swap(pieces, axis):
    return lax.all_to_all(pieces, axis, 0, 0, tiled=True)


def local(coeff, bank, alpha_tiles, alpha_blocks, alpha_count, beta_tiles, beta_blocks, beta_count):
    tile = coeff.shape[0]
    banks = bank.shape[0]
    n_row = lax.axis_size("row")
    n_col = lax.axis_size("col")
    slots = alpha_tiles.shape[1]
    alpha_in = swap(pack(coeff, n_row, True), "row")
    beta_in = swap(pack(coeff, n_col, False), "col")
    cap = (jnp.max(jnp.abs(bank)).astype(jnp.float32) * (slots * tile)).reshape(1)
    alpha_at = find(alpha_tiles, alpha_blocks, alpha_count, banks)
    beta_at = find(beta_tiles, beta_blocks, beta_count, banks)
    alpha_mix, alpha_unit = mix(alpha_in, bank, alpha_at, cap)
    beta_mix, beta_unit = mix(beta_in, bank, beta_at, cap)
    alpha_out = swap(alpha_mix, "row")
    beta_out = swap(beta_mix, "col")
    base = turn(alpha_out, alpha_unit, tile)
    return join(base, beta_out, beta_unit)


def solution(mesh):
    return jax.shard_map(
        local,
        mesh=mesh,
        in_specs=(P("row", "col"), P(), P(), P(), P(), P(), P(), P()),
        out_specs=P("row", "col"),
        check_vma=False,
    )
```

```python
import jax
import jax.numpy as jnp
from jax import lax
from jax.experimental import pallas as pl
from jax.experimental.pallas import tpu as pltpu
from jax.sharding import PartitionSpec as P

LANE = 128
PAD = 16
FOOT = 2
PAIR = 2
CHAINS = 2
ROOM = 24 << 20
VMEM = pl.BlockSpec(memory_space=pltpu.VMEM)
SMEM = pl.BlockSpec(memory_space=pltpu.SMEM)


def inside(x):
    return pltpu.with_memory_space_constraint(x, pltpu.VMEM)


def blocks_of(width, tile):
    return width * tile // LANE


def ship(flat, parts, axis, fold):
    rows = flat.shape[0] // parts
    moved = lax.all_to_all(flat.reshape(parts, rows // fold, fold, LANE), axis, 0, 0, tiled=True)
    return moved.reshape(flat.shape)


def pack_kernel(x_ref, out_ref, src_ref, top_ref, *, parts, flip):
    step = pl.program_id(0)
    tile = x_ref.shape[0]
    width = tile // parts
    used = blocks_of(width, tile)
    rows = out_ref.shape[0] // parts
    x = x_ref[...]
    level = jnp.max(jnp.abs(x.astype(jnp.float32)), axis=0, keepdims=True)
    top_ref[...] = jnp.where(step == 0, level, jnp.maximum(top_ref[...], level))
    if flip:
        src_ref[pl.ds(pl.multiple_of(step * LANE, LANE), LANE), :] = x.astype(jnp.float32).T.astype(x.dtype)
    else:
        src_ref[:, pl.ds(pl.multiple_of(step * LANE, LANE), LANE)] = x

    @pl.when(step == pl.num_programs(0) - 1)
    def _():
        top = jnp.max(top_ref[...], axis=1, keepdims=True)
        foot = jnp.broadcast_to(top, (rows - used, LANE)).astype(out_ref.dtype)
        for t in range(parts):
            for block in range(tile // LANE):
                out_ref[t * rows + block * width : t * rows + (block + 1) * width, :] = src_ref[
                    t * width : (t + 1) * width, block * LANE : (block + 1) * LANE
                ]
            out_ref[t * rows + used : (t + 1) * rows, :] = foot


def pack(piece, parts, flip):
    tile = piece.shape[0]
    shape = (parts * (blocks_of(tile // parts, tile) + FOOT), LANE)
    return pl.pallas_call(
        lambda *refs: pack_kernel(*refs, parts=parts, flip=flip),
        grid=(tile // LANE,),
        out_shape=jax.ShapeDtypeStruct(shape, piece.dtype),
        in_specs=[pl.BlockSpec((tile, LANE), lambda i: (0, i))],
        out_specs=pl.BlockSpec(shape, lambda i: (0, 0)),
        scratch_shapes=[pltpu.VMEM((tile, tile), piece.dtype), pltpu.VMEM((1, LANE), jnp.float32)],
        compiler_params=pltpu.CompilerParams(vmem_limit_bytes=ROOM),
        name="pack_flip" if flip else "pack",
    )(pltpu.with_memory_space_constraint(piece, pltpu.HBM))


def mix_kernel(places, cap, in_ref, bank_hbm, out_ref, scale_ref, x_ref, prod_ref, bank_ref, sems):
    banks, tile, _ = bank_ref.shape
    lanes = x_ref.shape[0]
    parts = lanes // PAD
    width = tile // parts
    used = blocks_of(width, tile)
    rows = used + FOOT
    edges = [0, PAIR, banks // 2, banks]
    copies = {
        low: pltpu.make_async_copy(bank_hbm.at[pl.ds(low, high - low)], bank_ref.at[pl.ds(low, high - low)], sems.at[i])
        for i, (low, high) in enumerate(zip(edges[:-1], edges[1:]))
    }
    for copy in copies.values():
        copy.start()

    x_ref[...] = jnp.zeros(x_ref.shape, x_ref.dtype)

    top = jnp.zeros((1, LANE), jnp.float32)
    for t in range(parts):
        for block in range(tile // LANE):
            x_ref[t * PAD : t * PAD + width, block * LANE : (block + 1) * LANE] = in_ref[
                t * rows + block * width : t * rows + (block + 1) * width, :
            ]
        foot = in_ref[t * rows + used : (t + 1) * rows, :].astype(jnp.float32)
        top = jnp.maximum(top, foot[:1])
    scale = 32768.0 / jnp.maximum(top * cap[0], 1e-30)
    scale_ref[...] = 1.0 / scale
    prod_ref[pl.ds(banks * lanes, PAD), :] = jnp.zeros((PAD, tile), jnp.float32)

    for b in range(0, banks, PAIR):
        if b in copies:
            copies[b].wait()
        both = lax.dot_general(
            x_ref[...],
            bank_ref[b : b + PAIR].reshape(PAIR * tile, tile),
            (((1,), (1,)), ((), ())),
            preferred_element_type=jnp.float32,
        )
        for side in range(PAIR):
            prod_ref[pl.ds((b + side) * lanes, lanes), :] = both[:, side * tile : (side + 1) * tile]

    def gather(pair, carry):
        out = out_ref.at[pl.ds(pl.multiple_of(pair * (PAIR * used), PAIR * used), PAIR * used), :]
        for side in range(PAIR):
            totals = [None] * CHAINS
            for slot in range(places.shape[1]):
                piece = prod_ref[pl.ds(pl.multiple_of(places[pair * PAIR + side, slot], PAD), PAD), :]
                chain = slot % CHAINS
                totals[chain] = piece if totals[chain] is None else totals[chain] + piece
            total = sum(totals[1:], totals[0])
            for block in range(tile // LANE):
                out[side * used + block * width : side * used + (block + 1) * width, :] = (
                    total[:width, block * LANE : (block + 1) * LANE] * scale
                )
        return carry

    lax.fori_loop(0, parts // PAIR, gather, 0)


def mix(pieces, bank, places, cap):
    parts = places.shape[0]
    banks, tile, _ = bank.shape
    out, unscale = pl.pallas_call(
        mix_kernel,
        out_shape=(
            jax.ShapeDtypeStruct((parts * blocks_of(tile // parts, tile), LANE), jnp.float32),
            jax.ShapeDtypeStruct((1, LANE), jnp.float32),
        ),
        in_specs=[SMEM, SMEM, VMEM, pl.BlockSpec(memory_space=pltpu.HBM)],
        out_specs=(VMEM, VMEM),
        scratch_shapes=[
            pltpu.VMEM((parts * PAD, tile), pieces.dtype),
            pltpu.VMEM((banks * parts * PAD + PAD, tile), jnp.float32),
            pltpu.VMEM(bank.shape, bank.dtype),
            pltpu.SemaphoreType.DMA((3,)),
        ],
        compiler_params=pltpu.CompilerParams(vmem_limit_bytes=ROOM),
        name="mix",
    )(places, cap, inside(pieces), pltpu.with_memory_space_constraint(bank, pltpu.HBM))
    return out.astype(jnp.float16), unscale


def find(tiles, blocks, count, banks):
    rows, slots = tiles.shape
    at = blocks * (rows * PAD) + tiles * PAD
    return jnp.where(jnp.arange(slots) < count[:, None], at, banks * rows * PAD)


def piece_of(parts_ref, t, block, width, used):
    return parts_ref[t * used + block * width : t * used + (block + 1) * width, :]


def turn_kernel(parts_ref, unit, out_ref, flip_ref, *, parts):
    tile = out_ref.shape[0]
    width = tile // parts
    for t in range(parts):
        for block in range(tile // LANE):
            flip_ref[t * width : (t + 1) * width, block * LANE : (block + 1) * LANE] = piece_of(
                parts_ref, t, block, width, blocks_of(width, tile)
            )
    out_ref[...] = flip_ref[...].T * unit[0, 0]


def turn(flat, unit, parts, tile):
    return pl.pallas_call(
        lambda *refs: turn_kernel(*refs, parts=parts),
        out_shape=jax.ShapeDtypeStruct((tile, tile), jnp.float32),
        in_specs=[VMEM, SMEM],
        out_specs=VMEM,
        scratch_shapes=[pltpu.VMEM((tile, tile), jnp.float32)],
        compiler_params=pltpu.CompilerParams(vmem_limit_bytes=ROOM),
        name="turn",
    )(inside(flat.astype(jnp.float32)), unit)


def join_kernel(base_ref, parts_ref, unit, out_ref, *, parts):
    tile = out_ref.shape[0]
    width = tile // parts
    for t in range(parts):
        for block in range(tile // LANE):
            rows, cols = slice(t * width, (t + 1) * width), slice(block * LANE, (block + 1) * LANE)
            piece = piece_of(parts_ref, t, block, width, blocks_of(width, tile))
            out_ref[rows, cols] = base_ref[rows, cols] + piece * unit[0, 0]


def join(base, flat, unit, parts):
    return pl.pallas_call(
        lambda *refs: join_kernel(*refs, parts=parts),
        out_shape=jax.ShapeDtypeStruct(base.shape, jnp.float32),
        in_specs=[VMEM, VMEM, SMEM],
        out_specs=VMEM,
        compiler_params=pltpu.CompilerParams(vmem_limit_bytes=ROOM, allow_input_fusion=[False, True, False]),
        name="join",
    )(inside(base), flat.astype(jnp.float32), unit)


def local(coeff, bank, alpha_tiles, alpha_blocks, alpha_count, beta_tiles, beta_blocks, beta_count):
    tile = coeff.shape[0]
    banks = bank.shape[0]
    n_row = lax.axis_size("row")
    n_col = lax.axis_size("col")
    slots = alpha_tiles.shape[1]
    alpha_in = ship(pack(coeff, n_row, True), n_row, "row", FOOT)
    beta_in = ship(pack(coeff, n_col, False), n_col, "col", FOOT)
    cap = (jnp.max(jnp.abs(bank)).astype(jnp.float32) * (slots * tile)).reshape(1)
    alpha_at = find(alpha_tiles, alpha_blocks, alpha_count, banks)
    beta_at = find(beta_tiles, beta_blocks, beta_count, banks)
    alpha_mix, alpha_unit = mix(alpha_in, bank, alpha_at, cap)
    beta_mix, beta_unit = mix(beta_in, bank, beta_at, cap)
    alpha_out = ship(alpha_mix, n_row, "row", 2 * FOOT)
    beta_out = ship(beta_mix, n_col, "col", 2 * FOOT)
    base = turn(alpha_out, alpha_unit, n_row, tile)
    return join(base, beta_out, beta_unit, n_col)


def solution(mesh):
    return jax.shard_map(
        local,
        mesh=mesh,
        in_specs=(P("row", "col"), P(), P(), P(), P(), P(), P(), P()),
        out_specs=P("row", "col"),
        check_vma=False,
    )
```

```python
import jax
import jax.numpy as jnp
from jax import lax
from jax.experimental import pallas as pl
from jax.experimental.pallas import tpu as pltpu
from jax.sharding import PartitionSpec as P

LANE = 128
PAD = 16
FOOT = 2
PAIR = 2
CHAINS = 2
ROOM = 24 << 20
VMEM = pl.BlockSpec(memory_space=pltpu.VMEM)
SMEM = pl.BlockSpec(memory_space=pltpu.SMEM)


def inside(x):
    return pltpu.with_memory_space_constraint(x, pltpu.VMEM)


def blocks_of(width, tile):
    return width * tile // LANE


def ship(flat, parts, axis, fold):
    rows = flat.shape[0] // parts
    moved = lax.all_to_all(flat.reshape(parts, rows // fold, fold, LANE), axis, 0, 0, tiled=True)
    return moved.reshape(flat.shape)


def pack_kernel(x_ref, out_ref, flip_ref, *, parts, flip):
    tile = x_ref.shape[0]
    width = tile // parts
    used = blocks_of(width, tile)
    rows = out_ref.shape[0] // parts
    x = x_ref[...]
    top = jnp.max(jnp.max(jnp.abs(x.astype(jnp.float32)), axis=0, keepdims=True), axis=1, keepdims=True)
    foot = jnp.broadcast_to(top, (rows - used, LANE)).astype(out_ref.dtype)
    if flip:
        flip_ref[...] = x.astype(jnp.float32).T.astype(x.dtype)
        src = flip_ref
    else:
        src = x_ref
    for t in range(parts):
        for block in range(tile // LANE):
            out_ref[t * rows + block * width : t * rows + (block + 1) * width, :] = src[
                t * width : (t + 1) * width, block * LANE : (block + 1) * LANE
            ]
        out_ref[t * rows + used : (t + 1) * rows, :] = foot


def pack(piece, parts, flip):
    tile = piece.shape[0]
    return pl.pallas_call(
        lambda *refs: pack_kernel(*refs, parts=parts, flip=flip),
        out_shape=jax.ShapeDtypeStruct((parts * (blocks_of(tile // parts, tile) + FOOT), LANE), piece.dtype),
        in_specs=[VMEM],
        out_specs=VMEM,
        scratch_shapes=[pltpu.VMEM((tile, tile), piece.dtype)],
        compiler_params=pltpu.CompilerParams(vmem_limit_bytes=ROOM),
        name="pack_flip" if flip else "pack",
    )(piece)


def mix_kernel(places, cap, in_ref, bank_hbm, out_ref, scale_ref, x_ref, prod_ref, bank_ref, sems):
    banks, tile, _ = bank_ref.shape
    lanes = x_ref.shape[0]
    parts = lanes // PAD
    width = tile // parts
    used = blocks_of(width, tile)
    rows = used + FOOT
    edges = [0, PAIR, banks // 2, banks]
    copies = {
        low: pltpu.make_async_copy(bank_hbm.at[pl.ds(low, high - low)], bank_ref.at[pl.ds(low, high - low)], sems.at[i])
        for i, (low, high) in enumerate(zip(edges[:-1], edges[1:]))
    }
    for copy in copies.values():
        copy.start()

    x_ref[...] = jnp.zeros(x_ref.shape, x_ref.dtype)

    top = jnp.zeros((1, LANE), jnp.float32)
    for t in range(parts):
        for block in range(tile // LANE):
            x_ref[t * PAD : t * PAD + width, block * LANE : (block + 1) * LANE] = in_ref[
                t * rows + block * width : t * rows + (block + 1) * width, :
            ]
        foot = in_ref[t * rows + used : (t + 1) * rows, :].astype(jnp.float32)
        top = jnp.maximum(top, foot[:1])
    scale = 32768.0 / jnp.maximum(top * cap[0], 1e-30)
    scale_ref[...] = 1.0 / scale
    prod_ref[pl.ds(banks * lanes, PAD), :] = jnp.zeros((PAD, tile), jnp.float32)

    for b in range(0, banks, PAIR):
        if b in copies:
            copies[b].wait()
        both = lax.dot_general(
            x_ref[...],
            bank_ref[b : b + PAIR].reshape(PAIR * tile, tile),
            (((1,), (1,)), ((), ())),
            preferred_element_type=jnp.float32,
        )
        for side in range(PAIR):
            prod_ref[pl.ds((b + side) * lanes, lanes), :] = both[:, side * tile : (side + 1) * tile]

    def gather(pair, carry):
        out = out_ref.at[pl.ds(pl.multiple_of(pair * (PAIR * used), PAIR * used), PAIR * used), :]
        for side in range(PAIR):
            totals = [None] * CHAINS
            for slot in range(places.shape[1]):
                piece = prod_ref[pl.ds(pl.multiple_of(places[pair * PAIR + side, slot], PAD), PAD), :]
                chain = slot % CHAINS
                totals[chain] = piece if totals[chain] is None else totals[chain] + piece
            total = sum(totals[1:], totals[0])
            for block in range(tile // LANE):
                out[side * used + block * width : side * used + (block + 1) * width, :] = (
                    total[:width, block * LANE : (block + 1) * LANE] * scale
                )
        return carry

    lax.fori_loop(0, parts // PAIR, gather, 0)


def mix(pieces, bank, places, cap):
    parts = places.shape[0]
    banks, tile, _ = bank.shape
    out, unscale = pl.pallas_call(
        mix_kernel,
        out_shape=(
            jax.ShapeDtypeStruct((parts * blocks_of(tile // parts, tile), LANE), jnp.float32),
            jax.ShapeDtypeStruct((1, LANE), jnp.float32),
        ),
        in_specs=[SMEM, SMEM, VMEM, pl.BlockSpec(memory_space=pltpu.HBM)],
        out_specs=(VMEM, VMEM),
        scratch_shapes=[
            pltpu.VMEM((parts * PAD, tile), pieces.dtype),
            pltpu.VMEM((banks * parts * PAD + PAD, tile), jnp.float32),
            pltpu.VMEM(bank.shape, bank.dtype),
            pltpu.SemaphoreType.DMA((3,)),
        ],
        compiler_params=pltpu.CompilerParams(vmem_limit_bytes=ROOM),
        name="mix",
    )(places, cap, inside(pieces), pltpu.with_memory_space_constraint(bank, pltpu.HBM))
    return out.astype(jnp.float16), unscale


def find(tiles, blocks, count, banks):
    rows, slots = tiles.shape
    at = blocks * (rows * PAD) + tiles * PAD
    return jnp.where(jnp.arange(slots) < count[:, None], at, banks * rows * PAD)


def piece_of(parts_ref, t, block, width, used):
    return parts_ref[t * used + block * width : t * used + (block + 1) * width, :]


def turn_kernel(parts_ref, unit, out_ref, flip_ref, *, parts):
    tile = out_ref.shape[0]
    width = tile // parts
    for t in range(parts):
        for block in range(tile // LANE):
            flip_ref[t * width : (t + 1) * width, block * LANE : (block + 1) * LANE] = piece_of(
                parts_ref, t, block, width, blocks_of(width, tile)
            )
    out_ref[...] = flip_ref[...].T * unit[0, 0]


def turn(flat, unit, parts, tile):
    return pl.pallas_call(
        lambda *refs: turn_kernel(*refs, parts=parts),
        out_shape=jax.ShapeDtypeStruct((tile, tile), jnp.float32),
        in_specs=[VMEM, SMEM],
        out_specs=VMEM,
        scratch_shapes=[pltpu.VMEM((tile, tile), jnp.float32)],
        compiler_params=pltpu.CompilerParams(vmem_limit_bytes=ROOM),
        name="turn",
    )(inside(flat.astype(jnp.float32)), unit)


def join_kernel(base_ref, parts_ref, unit, out_ref, *, parts):
    tile = out_ref.shape[0]
    width = tile // parts
    for t in range(parts):
        for block in range(tile // LANE):
            rows, cols = slice(t * width, (t + 1) * width), slice(block * LANE, (block + 1) * LANE)
            piece = piece_of(parts_ref, t, block, width, blocks_of(width, tile))
            out_ref[rows, cols] = base_ref[rows, cols] + piece * unit[0, 0]


def join(base, flat, unit, parts):
    return pl.pallas_call(
        lambda *refs: join_kernel(*refs, parts=parts),
        out_shape=jax.ShapeDtypeStruct(base.shape, jnp.float32),
        in_specs=[VMEM, VMEM, SMEM],
        out_specs=VMEM,
        compiler_params=pltpu.CompilerParams(vmem_limit_bytes=ROOM, allow_input_fusion=[False, True, False]),
        name="join",
    )(inside(base), flat.astype(jnp.float32), unit)


def local(coeff, bank, alpha_tiles, alpha_blocks, alpha_count, beta_tiles, beta_blocks, beta_count):
    tile = coeff.shape[0]
    banks = bank.shape[0]
    n_row = lax.axis_size("row")
    n_col = lax.axis_size("col")
    slots = alpha_tiles.shape[1]
    alpha_in = ship(pack(coeff, n_row, True), n_row, "row", FOOT)
    beta_in = ship(pack(coeff, n_col, False), n_col, "col", FOOT)
    cap = (jnp.max(jnp.abs(bank)).astype(jnp.float32) * (slots * tile)).reshape(1)
    alpha_at = find(alpha_tiles, alpha_blocks, alpha_count, banks)
    beta_at = find(beta_tiles, beta_blocks, beta_count, banks)
    alpha_mix, alpha_unit = mix(alpha_in, bank, alpha_at, cap)
    beta_mix, beta_unit = mix(beta_in, bank, beta_at, cap)
    alpha_out = ship(alpha_mix, n_row, "row", 2 * FOOT)
    beta_out = ship(beta_mix, n_col, "col", 2 * FOOT)
    base = turn(alpha_out, alpha_unit, n_row, tile)
    return join(base, beta_out, beta_unit, n_col)


def solution(mesh):
    return jax.shard_map(
        local,
        mesh=mesh,
        in_specs=(P("row", "col"), P(), P(), P(), P(), P(), P(), P()),
        out_specs=P("row", "col"),
        check_vma=False,
    )
```
